32 devices in a mesh: row: 4 (over z), col: 8 (over y, x, core).
Axes of the slice: x: 2, y: 2, z: 4, core: 2. Of those that a mesh axis runs over, the one named last changes fastest.
Arguments:
- state_start: bfloat16 [512, 2048], P('row', 'col'), may hold values from -360 to 360
- actions: int32 [512, 2], P('row'), may hold values from 0 to 17
- targets: bfloat16 [2, 512, 2048], P(None, 'row'), may hold values from -504 to 504
- w_in: bfloat16 [2048, 4096], P('row', 'col'), may hold values from -0.125 to 0.125
- w_out: bfloat16 [4096, 2048], P('col', 'row'), may hold values from -0.09375 to 0.09375
- action_embed: bfloat16 [18, 4096], P(None, 'col'), may hold values from -6 to 6
Outputs:
- grad_w_in: float32 [2048, 4096], P('row', 'col')
- grad_w_out: float32 [4096, 2048], P('col', 'row')
The draws below stay inside these ranges and needn't reach their ends.
All inputs are finite; a program needn't handle non-finite values.
Results may differ from the reference program's by a relative error of at most 0.035.
Values may be sent and summed in bfloat16 or wider, within the bound.
A program may use at most 64 MiB of HBM per device.

```python
import math
import jax
import jax.numpy as jnp
from jax import lax

D = 2048
FF = 4096
ACTIONS = 18
UNROLL = 2
ROWS = 512
N_COL = 8


def joint_fields(key):
    row_key = jax.random.fold_in(key, 11)
    base_key = jax.random.fold_in(key, 12)
    noise_key = jax.random.fold_in(key, 13)
    row_scale = jnp.exp(jax.random.uniform(row_key, (ROWS, 1), jnp.float32, 0.0, math.log(10.0)))
    feature = jnp.arange(D, dtype=jnp.float32) / D
    col_scale = jnp.exp(math.log(3.0) * feature)[None, :]
    base = jnp.clip(jax.random.normal(base_key, (ROWS, D), jnp.float32), -4.0, 4.0)
    noise = jnp.clip(jax.random.normal(noise_key, (UNROLL, ROWS, D), jnp.float32), -4.0, 4.0)
    start = base * row_scale * col_scale
    target_field = 0.6 * start[None] + 0.8 * noise * row_scale[None] * col_scale[None]
    return (start, target_field)


def draw_state_start(key, part):
    start, target_field = joint_fields(key)
    return start.astype(jnp.bfloat16)


def draw_targets(key, part):
    start, target_field = joint_fields(key)
    return target_field.astype(jnp.bfloat16)


def touch_ends(entries, own_key, smallest, largest):
    longest = entries.shape.index(max(entries.shape))
    spots = []
    for shift in (0, 1):
        where = [jax.random.randint(jax.random.fold_in(own_key, axis), (), 0, length) for axis, length in enumerate(entries.shape)]
        where[longest] = (where[longest] + shift) % entries.shape[longest]
        spots.append(tuple(where))
    return entries.at[spots[0]].set(smallest).at[spots[1]].set(largest)


def level_of(rng, shape, split, smallest, largest):
    gain = 1.0
    for axis_at, shards_of in split:
        heights = jax.random.uniform(jax.random.fold_in(jax.random.fold_in(rng, 6), axis_at), (shards_of,), jnp.float32, smallest / len(split), largest / len(split))
        gain = gain * jnp.repeat(jnp.exp(heights), shape[axis_at] // shards_of).reshape((-1,) + (1,) * (len(shape) - 1 - axis_at))
    return gain


def centred(own_key, extent, width, reach, cuts=(), held_as=jnp.bfloat16):
    entries = width * jax.random.normal(own_key, extent, jnp.float32)
    if cuts:
        entries = entries * level_of(own_key, extent, cuts, -0.22, 0.18)
    return jnp.clip(entries, -reach, reach).astype(held_as)


def setup_inputs(seed: int = 0) -> dict:
    splits = jax.random.split(jax.random.key(seed), 7)
    state_start = draw_state_start(jax.random.fold_in(splits[6], 71), 0)
    actions = touch_ends(jax.random.randint(splits[1], (ROWS, UNROLL), 0, ACTIONS), jax.random.fold_in(splits[1], 1), 0, ACTIONS - 1).astype(jnp.int32)
    targets = draw_targets(jax.random.fold_in(splits[6], 71), 0)
    w_in = centred(splits[3], (D, FF), D ** -0.5, 0.125, ((0, 4), (1, 8)))
    w_out = centred(splits[4], (FF, D), FF ** -0.5, 0.09375, ((0, 8), (1, 4)))
    action_embed = centred(splits[5], (ACTIONS, FF), 1.0, 6.0, ((1, 8),))
    return dict(state_start=state_start, actions=actions, targets=targets, w_in=w_in, w_out=w_out, action_embed=action_embed)


EPS = 1e-06
LOSS_SCALE = 128.0

def silu_grad(pre_act):
    gate_val = jax.nn.sigmoid(pre_act)
    return gate_val * (1.0 + pre_act * (1.0 - gate_val))

def cosine_grad(state, target):
    state_f = state.astype(jnp.float32)
    target_f = target.astype(jnp.float32)
    self_dot = lax.optimization_barrier(jnp.sum(state_f * state_f, axis=-1, keepdims=True))
    cross_dot = lax.optimization_barrier(jnp.sum(state_f * target_f, axis=-1, keepdims=True))
    target_dot = lax.optimization_barrier(jnp.sum(target_f * target_f, axis=-1, keepdims=True))
    inv_state = lax.rsqrt(self_dot + EPS)
    inv_target = lax.rsqrt(target_dot + EPS)
    cosine = cross_dot * inv_state * inv_target
    return -LOSS_SCALE * (target_f * inv_state * inv_target - cosine * state_f * inv_state * inv_state)

def group_sum(left_groups, right_groups):

    def add_group(summed, operands):
        left_part, right_part = operands
        term = jnp.dot(left_part, right_part, preferred_element_type=jnp.float32).astype(jnp.bfloat16)
        term = lax.optimization_barrier(term)
        return (summed + term.astype(jnp.float32), None)
    init = jnp.zeros((left_groups.shape[0], right_groups.shape[2]), jnp.float32)
    summed, _ = lax.scan(add_group, init, (jnp.transpose(left_groups, (1, 0, 2)), right_groups))
    return summed

def reference(state_start, actions, targets, w_in, w_out, action_embed):
    hidden_cols = FF // N_COL
    w_in_groups = jnp.transpose(w_in.reshape(D, N_COL, hidden_cols), (1, 2, 0))
    w_out_groups = w_out.reshape(N_COL, hidden_cols, D)
    action_ids = jnp.arange(ACTIONS, dtype=jnp.int32)
    states = [state_start]
    pre_list = []
    hidden_list = []
    for unroll in range(UNROLL):
        current = states[-1]
        onehot = (actions[:, unroll][:, None] == action_ids[None, :]).astype(jnp.bfloat16)
        pre_act = jnp.dot(current, w_in, preferred_element_type=jnp.float32) + jnp.dot(onehot, action_embed, preferred_element_type=jnp.float32)
        hidden = jax.nn.silu(pre_act).astype(jnp.bfloat16)
        branch = group_sum(hidden.reshape(ROWS, N_COL, hidden_cols), w_out_groups)
        states.append((current.astype(jnp.float32) + branch).astype(jnp.bfloat16))
        pre_list.append(pre_act)
        hidden_list.append(hidden)
    state_grad = cosine_grad(states[UNROLL], targets[UNROLL - 1]).astype(jnp.bfloat16)
    grad_w_in = jnp.zeros((D, FF), jnp.float32)
    grad_w_out = jnp.zeros((FF, D), jnp.float32)
    for unroll in reversed(range(UNROLL)):
        back = jnp.dot(state_grad, w_out.T, preferred_element_type=jnp.float32)
        hid_grad = (back * silu_grad(pre_list[unroll])).astype(jnp.bfloat16)
        grad_w_out = grad_w_out + jnp.dot(hidden_list[unroll].T, state_grad, preferred_element_type=jnp.float32)
        grad_w_in = grad_w_in + jnp.dot(states[unroll].T, hid_grad, preferred_element_type=jnp.float32)
        if unroll > 0:
            input_part = group_sum(hid_grad.reshape(ROWS, N_COL, hidden_cols), w_in_groups)
            state_grad = (state_grad.astype(jnp.float32) + input_part + cosine_grad(states[unroll], targets[unroll - 1])).astype(jnp.bfloat16)
    return (grad_w_in, grad_w_out)
```

```python
import functools

import jax
import jax.numpy as jnp
from jax import lax
from jax.experimental import pallas as pl
from jax.experimental.pallas import tpu as pltpu
from jax.sharding import PartitionSpec as P

EPS = 1e-06
LOSS_SCALE = 128.0
MESH = pl.DeviceIdType.MESH
F32 = jnp.float32
BF16 = jnp.bfloat16


def silu_grad(pre_act):
    gate_val = jax.nn.sigmoid(pre_act)
    return gate_val * (1.0 + pre_act * (1.0 - gate_val))


def cosine_from(state_f, target_f, self_dot, cross_dot, target_dot):
    inv_state = lax.rsqrt(self_dot + EPS)
    inv_target = lax.rsqrt(target_dot + EPS)
    cosine = cross_dot * inv_state * inv_target
    return -LOSS_SCALE * (
        target_f * inv_state * inv_target - cosine * state_f * inv_state * inv_state
    )


def shared_cosine(state, target):
    state_f = state.astype(jnp.float32)
    target_f = target.astype(jnp.float32)
    self_dot, cross_dot, target_dot = lax.psum(
        (
            jnp.sum(state_f * state_f, axis=-1),
            jnp.sum(state_f * target_f, axis=-1),
            jnp.sum(target_f * target_f, axis=-1),
        ),
        "col",
    )
    return cosine_from(
        state_f, target_f, self_dot[:, None], cross_dot[:, None], target_dot[:, None]
    )


def gathered(state_start, actions, targets, w_in, w_out, action_embed):
    unroll_steps = targets.shape[0]
    col_width = state_start.shape[1]
    w_in_panel = lax.all_gather(w_in, "row", axis=0, tiled=True)
    w_out_panel = lax.all_gather(w_out, "row", axis=1, tiled=True)
    col_start = lax.axis_index("col") * col_width
    action_ids = jnp.arange(action_embed.shape[0], dtype=jnp.int32)
    contract_last = (((1,), (1,)), ((), ()))
    current = state_start
    full_states = []
    pre_list = []
    hidden_list = []
    cos_terms = []
    for unroll in range(unroll_steps):
        full_rows = lax.all_gather(current, "col", axis=1, tiled=True)
        onehot = (actions[:, unroll][:, None] == action_ids[None, :]).astype(jnp.bfloat16)
        pre_act = jnp.dot(full_rows, w_in_panel, preferred_element_type=jnp.float32) + jnp.dot(
            onehot, action_embed, preferred_element_type=jnp.float32
        )
        hidden = jax.nn.silu(pre_act).astype(jnp.bfloat16)
        partial_value = jnp.dot(hidden, w_out_panel, preferred_element_type=jnp.float32)
        target = targets[unroll]
        branch = lax.psum_scatter(
            partial_value.astype(jnp.bfloat16), "col", scatter_dimension=1, tiled=True
        ).astype(jnp.float32)
        current = (current.astype(jnp.float32) + branch).astype(jnp.bfloat16)
        target_slice = lax.dynamic_slice_in_dim(target, col_start, col_width, 1)
        cos_terms.append(shared_cosine(current, target_slice))
        full_states.append(full_rows)
        pre_list.append(pre_act)
        hidden_list.append(hidden)
    state_grad = cos_terms[unroll_steps - 1].astype(jnp.bfloat16)
    grad_list = [None] * unroll_steps
    hid_grads = [None] * unroll_steps
    for unroll in reversed(range(unroll_steps)):
        grad_rows = lax.all_gather(state_grad, "col", axis=1, tiled=True)
        back = lax.dot_general(
            grad_rows, w_out_panel, contract_last, preferred_element_type=jnp.float32
        )
        hid_grad = (back * silu_grad(pre_list[unroll])).astype(jnp.bfloat16)
        grad_list[unroll] = grad_rows
        hid_grads[unroll] = hid_grad
        if unroll > 0:
            input_part = lax.dot_general(
                hid_grad, w_in_panel, contract_last, preferred_element_type=jnp.float32
            )
            summed = lax.psum_scatter(
                input_part.astype(jnp.bfloat16), "col", scatter_dimension=1, tiled=True
            ).astype(jnp.float32)
            state_grad = (state_grad.astype(jnp.float32) + summed + cos_terms[unroll - 1]).astype(
                jnp.bfloat16
            )
    grad_stack = jnp.stack(grad_list)
    hidden_stack = jnp.stack(hidden_list)
    state_stack = jnp.stack(full_states)
    hid_stack = jnp.stack(hid_grads)
    grad_feature_blocks = lax.all_to_all(grad_stack, "row", split_axis=2, concat_axis=1, tiled=True)
    hidden_all = lax.all_gather(hidden_stack, "row", axis=1, tiled=True)
    grad_w_out = jnp.einsum(
        "kbf,kbd->fd", hidden_all, grad_feature_blocks, preferred_element_type=jnp.float32
    )
    state_feature_blocks = lax.all_to_all(
        state_stack, "row", split_axis=2, concat_axis=1, tiled=True
    )
    hid_all = lax.all_gather(hid_stack, "row", axis=1, tiled=True)
    grad_w_in = jnp.einsum(
        "kbd,kbf->df", state_feature_blocks, hid_all, preferred_element_type=jnp.float32
    )
    return (grad_w_in, grad_w_out)


def sem_plan(nr, nc):
    at = {}
    total = 0
    for name, count in (
        [("start", 2 * nr), ("targets", nr)]
        + [(f"cag{i}", nr * nc) for i in range(4)]
        + [(f"zrs{i}", nr) for i in range(4)]
        + [(f"zag{i}", nr) for i in range(4)]
        + [(f"crs{i}", nr * nc) for i in range(3)]
        + [(f"dot{i}", nr) for i in range(2)]
    ):
        at[name] = total
        total += count
    return at, total


def sends_in_all(nr, nc):
    return nc + (nr - 1) * (1 + 4 + 4 + 2) + (4 + 3) * nr * (nc - 1)


def kernel(
    nr, nc, st, act, tg, wi, wo, emb, gwi, gwo,
    s0p, tgp, sfull, hfull, efull, gfull, psend, zr, ysend, cr, own, pre, dsend, dz,
    send_sem, recv_sem,
):
    r, c = lax.axis_index("row"), lax.axis_index("col")
    piece, df = sfull.shape[3], sfull.shape[4]
    rb = nc * piece
    at, _ = sem_plan(nr, nc)
    started = []
    unused = iter(range(10000))

    def zpeer(o):
        return lax.rem(r + o, nr)

    def cpeer(o):
        return lax.rem(c + o, nc)

    def copy(src, dst, sem, slot, dev):
        return pltpu.make_async_remote_copy(
            src_ref=src, dst_ref=dst, send_sem=send_sem.at[sem], recv_sem=recv_sem.at[slot],
            device_id=dev, device_id_type=MESH,
        )

    def send(src, dst, slot, dev):
        out = copy(src, dst, next(unused), slot, dev)
        out.start()
        started.append(out)

    def arrived(dst, slot, dev):
        copy(dst, dst, 0, slot, dev).wait_recv()

    barrier = pltpu.get_barrier_semaphore()
    for o in range(1, nr):
        pl.semaphore_signal(barrier, inc=1, device_id=(zpeer(o), c), device_id_type=MESH)
    for o in range(1, nc):
        pl.semaphore_signal(barrier, inc=1, device_id=(r, cpeer(o)), device_id_type=MESH)
    home = lax.div(c, 2)
    half = lax.rem(c, 2)
    for hf in range(2):
        for o in range(1, nr):
            pl.semaphore_signal(
                barrier, inc=1, device_id=(zpeer(o), 2 * r + hf), device_id_type=MESH
            )

        @pl.when(2 * r + hf != c)
        def _():
            pl.semaphore_signal(barrier, inc=1, device_id=(r, 2 * r + hf), device_id_type=MESH)

    away = jnp.where(home != r, 1, 0)
    pl.semaphore_wait(barrier, (nr - 1) + (nc - 1) + (nc - 1) + away)

    for o in range(1, nc):
        j = cpeer(o)
        send(st.at[j], s0p.at[half, r], at["start"] + half * nr + r, (home, j))
    keep = next(unused)

    @pl.when(home != r)
    def _():
        copy(st.at[c], s0p.at[half, r], keep, at["start"] + half * nr + r, (home, c)).start()

    @pl.when(home == r)
    def _():
        s0p[half, r] = st[c]

    for hf in range(2):
        for o in range(1, nr):
            b = zpeer(o)
            arrived(s0p.at[hf, b], at["start"] + hf * nr + b, (b, 2 * r + hf))

        @pl.when(2 * r + hf != c)
        def _():
            arrived(s0p.at[hf, r], at["start"] + hf * nr + r, (r, 2 * r + hf))

    order = [zpeer(o) for o in range(1, nr)] + [r]
    back_order = [r] + [zpeer(o) for o in range(1, nr)]

    def spread(full, name, b):
        for o in range(1, nc):
            send(full.at[b, c], full.at[b, c], at[name] + c * nr + b, (r, cpeer(o)))

    def collect(full, name, b):
        for o in range(1, nc):
            j = cpeer(o)
            arrived(full.at[b, j], at[name] + j * nr + b, (r, j))

    for b in order:
        sfull[0, b, c] = jnp.concatenate([s0p[0, b], s0p[1, b]], axis=-1)
        spread(sfull.at[0], "cag0", b)

    for o in range(1, nr):
        b = zpeer(o)
        send(
            tg.at[:, c, :, pl.ds(pl.multiple_of(b * df, df), df)],
            tgp.at[r], at["targets"] + r, (b, c),
        )
    tgp[r] = tg[:, c, :, pl.ds(pl.multiple_of(r * df, df), df)]

    def mm(a, b, dims=((1,), (0,))):
        return lax.dot_general(a, b, (dims, ((), ())), preferred_element_type=F32)

    def reduce_rows(full, name, weight, dims, phase):
        for o in range(1, nr):
            b = zpeer(o)
            collect(full, name, b)
            term = mm(full[b].reshape(rb, df), weight[...], dims)
            psend[phase, b] = term.astype(BF16)
            send(psend.at[phase, b], zr.at[phase, r], at[f"zrs{phase}"] + r, (b, c))
        collect(full, name, r)
        return mm(full[r].reshape(rb, df), weight[...], dims)

    def reduced(total, phase):
        for o in range(1, nr):
            b = zpeer(o)
            arrived(zr.at[phase, b], at[f"zrs{phase}"] + b, (b, c))
            total = total + zr[phase, b].astype(F32)
        return total

    def share_rows(full, phase):
        for o in range(1, nr):
            send(full.at[r], full.at[r], at[f"zag{phase}"] + r, (zpeer(o), c))

    def shared(full, phase, b):
        arrived(full.at[b], at[f"zag{phase}"] + b, (b, c))

    def group_terms(full, zphase, weight, dims, phase):
        for i, b in enumerate(back_order):
            if i:
                shared(full, zphase, b)
            term = mm(full[b], weight[...], dims).astype(BF16)
            ysend[phase, b] = term.reshape(nc, piece, df)
            for o in range(1, nc):
                j = cpeer(o)
                send(ysend.at[phase, b, j], cr.at[phase, b, c], at[f"crs{phase}"] + c * nr + b, (r, j))

    def group_total(phase, b):
        total = ysend[phase, b, c].astype(F32)
        for o in range(1, nc):
            j = cpeer(o)
            arrived(cr.at[phase, b, j], at[f"crs{phase}"] + j * nr + b, (r, j))
            total = total + cr[phase, b, j].astype(F32)
        return total

    lane = lax.broadcasted_iota(jnp.int32, (piece, 128), 1)

    def dots(u):
        for b in back_order:
            s = own[u, b].astype(F32)
            t = tgp[b, u].astype(F32)
            ss = jnp.sum(s * s, axis=-1, keepdims=True)
            sc = jnp.sum(s * t, axis=-1, keepdims=True)
            tt = jnp.sum(t * t, axis=-1, keepdims=True)
            both = jnp.where(lane == 0, ss, jnp.where(lane == 1, sc, tt))
            dsend[u, b] = both
        dz[u, r] = dsend[u]
        for o in range(1, nr):
            send(dsend.at[u], dz.at[u, r], at[f"dot{u}"] + r, (zpeer(o), c))

    def dots_in(u):
        for o in range(1, nr):
            b = zpeer(o)
            arrived(dz.at[u, b], at[f"dot{u}"] + b, (b, c))

    def cosine(u, b):
        total = dz[u, 0, b]
        for i in range(1, nr):
            total = total + dz[u, i, b]
        return cosine_from(
            own[u, b].astype(F32), tgp[b, u].astype(F32),
            total[:, 0:1], total[:, 1:2], total[:, 2:3],
        )

    ids = lax.broadcasted_iota(jnp.int32, (rb, emb.shape[0]), 1)
    plain, flipped, over_rows = ((1,), (0,)), ((1,), (1,)), ((0,), (0,))

    for u in range(2):
        total = reduce_rows(sfull.at[u], f"cag{u}", wi, plain, u)
        onehot = (act[:, u:u + 1] == ids).astype(F32).astype(BF16)
        total = total + mm(onehot, emb[...])
        if u == 1:
            dots(0)
        total = reduced(total, u)
        pre[u] = total
        hfull[u, r] = (total * jax.nn.sigmoid(total)).astype(BF16)
        share_rows(hfull.at[u], u)
        if u == 0:
            for o in range(1, nr):
                b = zpeer(o)
                arrived(tgp.at[b], at["targets"] + b, (b, c))
        group_terms(hfull.at[u], u, wo, plain, u)
        for b in back_order:
            new = (sfull[u, b, c].astype(F32) + group_total(u, b)).astype(BF16)
            own[u, b] = new
            if u == 0:
                sfull[1, b, c] = new
                spread(sfull.at[1], "cag1", b)

    dots(1)
    dots_in(1)
    for b in order:
        gfull[1, b, c] = cosine(1, b).astype(BF16)
        spread(gfull.at[1], "cag2", b)
    for u in (1, 0):
        total = reduce_rows(gfull.at[u], f"cag{3 - u}", wo, flipped, 3 - u)
        total = reduced(total, 3 - u)
        efull[u, r] = (total * silu_grad(pre[u])).astype(BF16)
        share_rows(efull.at[u], 3 - u)
        if u == 1:
            group_terms(efull.at[1], 2, wi, flipped, 2)
            dots_in(0)
            for b in back_order:
                summed = gfull[1, b, c].astype(F32) + group_total(2, b) + cosine(0, b)
                gfull[0, b, c] = summed.astype(BF16)
                spread(gfull.at[0], "cag3", b)
            gwo[...] = mm(hfull[1].reshape(nr * rb, -1), gfull[1].reshape(nr * rb, df), over_rows)
            gwi[...] = mm(sfull[1].reshape(nr * rb, df), efull[1].reshape(nr * rb, -1), over_rows)
    gwo[...] += mm(hfull[0].reshape(nr * rb, -1), gfull[0].reshape(nr * rb, df), over_rows)
    for b in order[:-1]:
        shared(efull.at[0], 3, b)
    gwi[...] += mm(sfull[0].reshape(nr * rb, df), efull[0].reshape(nr * rb, -1), over_rows)

    for out in started:
        out.wait_send()

    @pl.when(home != r)
    def _():
        copy(st.at[c], s0p.at[half, r], keep, at["start"] + half * nr + r, (home, c)).wait_send()


def stationary(nr, nc, state_start, actions, targets, w_in, w_out, action_embed):
    rb, sw = state_start.shape
    piece = rb // nc
    df, fc = w_in.shape
    vm = pl.BlockSpec(memory_space=pltpu.VMEM)
    _, receives = sem_plan(nr, nc)
    return pl.pallas_call(
        functools.partial(kernel, nr, nc),
        out_shape=(
            jax.ShapeDtypeStruct((df, fc), F32),
            jax.ShapeDtypeStruct((fc, df), F32),
        ),
        in_specs=[vm] * 6,
        out_specs=(vm, vm),
        scratch_shapes=[
            pltpu.VMEM((2, nr, piece, sw), BF16),
            pltpu.VMEM((nr, 2, piece, df), BF16),
            pltpu.VMEM((2, nr, nc, piece, df), BF16),
            pltpu.VMEM((2, nr, rb, fc), BF16),
            pltpu.VMEM((2, nr, rb, fc), BF16),
            pltpu.VMEM((2, nr, nc, piece, df), BF16),
            pltpu.VMEM((4, nr, rb, fc), BF16),
            pltpu.VMEM((4, nr, rb, fc), BF16),
            pltpu.VMEM((3, nr, nc, piece, df), BF16),
            pltpu.VMEM((3, nr, nc, piece, df), BF16),
            pltpu.VMEM((2, nr, piece, df), BF16),
            pltpu.VMEM((2, rb, fc), F32),
            pltpu.VMEM((2, nr, piece, 128), F32),
            pltpu.VMEM((2, nr, nr, piece, 128), F32),
            pltpu.SemaphoreType.DMA((sends_in_all(nr, nc),)),
            pltpu.SemaphoreType.DMA((receives,)),
        ],
        compiler_params=pltpu.CompilerParams(
            collective_id=0, has_side_effects=True, vmem_limit_bytes=56 * 1024 * 1024
        ),
    )(
        state_start.reshape(nc, piece, sw),
        actions,
        targets.reshape(targets.shape[0], nc, piece, targets.shape[2]),
        w_in,
        w_out,
        action_embed,
    )


def solution(mesh):
    nr, nc = mesh.shape["row"], mesh.shape["col"]

    def on_device(state_start, actions, targets, w_in, w_out, action_embed):
        rb, sw = state_start.shape
        fits = (
            targets.shape[0] == 2
            and nc == 2 * nr
            and rb % (16 * nc) == 0
            and sw % 128 == 0
            and w_in.shape[0] % 128 == 0
            and w_in.shape[1] % 128 == 0
        )
        args = (state_start, actions, targets, w_in, w_out, action_embed)
        if fits:
            return stationary(nr, nc, *args)
        return gathered(*args)

    in_specs = (
        P("row", "col"),
        P("row", None),
        P(None, "row", None),
        P("row", "col"),
        P("col", "row"),
        P(None, "col"),
    )
    out_specs = (P("row", "col"), P("col", "row"))
    return jax.shard_map(
        on_device, mesh=mesh, in_specs=in_specs, out_specs=out_specs, check_vma=False
    )
```

```python
import functools

import jax
import jax.numpy as jnp
from jax import lax
from jax.experimental import pallas as pl
from jax.experimental.pallas import tpu as pltpu
from jax.sharding import PartitionSpec as P

EPS = 1e-06
LOSS_SCALE = 128.0
MESH = pl.DeviceIdType.MESH
F32 = jnp.float32
BF16 = jnp.bfloat16


def silu_grad(pre_act):
    gate_val = jax.nn.sigmoid(pre_act)
    return gate_val * (1.0 + pre_act * (1.0 - gate_val))


def cosine_from(state_f, target_f, self_dot, cross_dot, target_dot):
    inv_state = lax.rsqrt(self_dot + EPS)
    inv_target = lax.rsqrt(target_dot + EPS)
    cosine = cross_dot * inv_state * inv_target
    return -LOSS_SCALE * (
        target_f * inv_state * inv_target - cosine * state_f * inv_state * inv_state
    )


def shared_cosine(state, target):
    state_f = state.astype(jnp.float32)
    target_f = target.astype(jnp.float32)
    self_dot, cross_dot, target_dot = lax.psum(
        (
            jnp.sum(state_f * state_f, axis=-1),
            jnp.sum(state_f * target_f, axis=-1),
            jnp.sum(target_f * target_f, axis=-1),
        ),
        "col",
    )
    return cosine_from(
        state_f, target_f, self_dot[:, None], cross_dot[:, None], target_dot[:, None]
    )


def gathered(state_start, actions, targets, w_in, w_out, action_embed):
    unroll_steps = targets.shape[0]
    col_width = state_start.shape[1]
    w_in_panel = lax.all_gather(w_in, "row", axis=0, tiled=True)
    w_out_panel = lax.all_gather(w_out, "row", axis=1, tiled=True)
    col_start = lax.axis_index("col") * col_width
    action_ids = jnp.arange(action_embed.shape[0], dtype=jnp.int32)
    contract_last = (((1,), (1,)), ((), ()))
    current = state_start
    full_states = []
    pre_list = []
    hidden_list = []
    cos_terms = []
    for unroll in range(unroll_steps):
        full_rows = lax.all_gather(current, "col", axis=1, tiled=True)
        onehot = (actions[:, unroll][:, None] == action_ids[None, :]).astype(jnp.bfloat16)
        pre_act = jnp.dot(full_rows, w_in_panel, preferred_element_type=jnp.float32) + jnp.dot(
            onehot, action_embed, preferred_element_type=jnp.float32
        )
        hidden = jax.nn.silu(pre_act).astype(jnp.bfloat16)
        partial_value = jnp.dot(hidden, w_out_panel, preferred_element_type=jnp.float32)
        target = targets[unroll]
        branch = lax.psum_scatter(
            partial_value.astype(jnp.bfloat16), "col", scatter_dimension=1, tiled=True
        ).astype(jnp.float32)
        current = (current.astype(jnp.float32) + branch).astype(jnp.bfloat16)
        target_slice = lax.dynamic_slice_in_dim(target, col_start, col_width, 1)
        cos_terms.append(shared_cosine(current, target_slice))
        full_states.append(full_rows)
        pre_list.append(pre_act)
        hidden_list.append(hidden)
    state_grad = cos_terms[unroll_steps - 1].astype(jnp.bfloat16)
    grad_list = [None] * unroll_steps
    hid_grads = [None] * unroll_steps
    for unroll in reversed(range(unroll_steps)):
        grad_rows = lax.all_gather(state_grad, "col", axis=1, tiled=True)
        back = lax.dot_general(
            grad_rows, w_out_panel, contract_last, preferred_element_type=jnp.float32
        )
        hid_grad = (back * silu_grad(pre_list[unroll])).astype(jnp.bfloat16)
        grad_list[unroll] = grad_rows
        hid_grads[unroll] = hid_grad
        if unroll > 0:
            input_part = lax.dot_general(
                hid_grad, w_in_panel, contract_last, preferred_element_type=jnp.float32
            )
            summed = lax.psum_scatter(
                input_part.astype(jnp.bfloat16), "col", scatter_dimension=1, tiled=True
            ).astype(jnp.float32)
            state_grad = (state_grad.astype(jnp.float32) + summed + cos_terms[unroll - 1]).astype(
                jnp.bfloat16
            )
    grad_stack = jnp.stack(grad_list)
    hidden_stack = jnp.stack(hidden_list)
    state_stack = jnp.stack(full_states)
    hid_stack = jnp.stack(hid_grads)
    grad_feature_blocks = lax.all_to_all(grad_stack, "row", split_axis=2, concat_axis=1, tiled=True)
    hidden_all = lax.all_gather(hidden_stack, "row", axis=1, tiled=True)
    grad_w_out = jnp.einsum(
        "kbf,kbd->fd", hidden_all, grad_feature_blocks, preferred_element_type=jnp.float32
    )
    state_feature_blocks = lax.all_to_all(
        state_stack, "row", split_axis=2, concat_axis=1, tiled=True
    )
    hid_all = lax.all_gather(hid_stack, "row", axis=1, tiled=True)
    grad_w_in = jnp.einsum(
        "kbd,kbf->df", state_feature_blocks, hid_all, preferred_element_type=jnp.float32
    )
    return (grad_w_in, grad_w_out)


def sem_plan(nr, nc):
    at = {}
    total = 0
    for name, count in (
        [("start", nr), ("targets", nr)]
        + [(f"cag{i}", nr * nc) for i in range(4)]
        + [(f"zrs{i}", 2 * nr) for i in range(4)]
        + [(f"zag{i}", 2 * nr) for i in range(4)]
        + [(f"crs{i}", nr * nc) for i in range(3)]
        + [(f"dot{i}", 2 * nr) for i in range(2)]
    ):
        at[name] = total
        total += count
    return at, total


def sends_in_all(nr, nc):
    per = nc // 2
    return per + (nr - 1) * (1 + 8 + 8 + 4) + 4 * nr * (nc - 1) + 3 * 2 * nr * per


def kernel(
    nr, nc, st, act, tg, wi, wo, emb, gwi, gwo,
    s0p, tgp, sfull, hfull, efull, gfull, psend, zr, ysend, cr, own, pre, dsend, dz,
    send_sem, recv_sem,
):
    r, c = lax.axis_index("row"), lax.axis_index("col")
    piece, df = sfull.shape[3], sfull.shape[4]
    per, pair = nc // 2, nr // 2
    rows = per * piece
    home, half = lax.div(c, 2), lax.rem(c, 2)
    place, first = lax.div(c, 2), half * pair
    side = lax.div(r, pair)
    at, _ = sem_plan(nr, nc)
    started = []
    unused = iter(range(10000))

    def zpeer(o):
        return lax.rem(r + o, nr)

    def cpeer(o):
        return lax.rem(c + o, nc)

    def copy(src, dst, sem, slot, dev):
        return pltpu.make_async_remote_copy(
            src_ref=src, dst_ref=dst, send_sem=send_sem.at[sem], recv_sem=recv_sem.at[slot],
            device_id=dev, device_id_type=MESH,
        )

    def send(src, dst, slot, dev, when=None):
        sem = next(unused)
        started.append((src, dst, sem, slot, dev, when))
        if when is None:
            copy(src, dst, sem, slot, dev).start()
        else:
            pl.when(when)(lambda: copy(src, dst, sem, slot, dev).start())

    def arrived(dst, slot, dev, when=None):
        if when is None:
            copy(dst, dst, 0, slot, dev).wait_recv()
        else:
            pl.when(when)(lambda: copy(dst, dst, 0, slot, dev).wait_recv())

    barrier = pltpu.get_barrier_semaphore()
    for o in range(1, nr):
        pl.semaphore_signal(barrier, inc=1, device_id=(zpeer(o), c), device_id_type=MESH)
    for o in range(1, nc):
        pl.semaphore_signal(barrier, inc=1, device_id=(r, cpeer(o)), device_id_type=MESH)
    for hf in range(2):
        for i in range(pair):

            @pl.when((2 * r + hf != c) | (first + i != r))
            def _():
                pl.semaphore_signal(
                    barrier, inc=1, device_id=(first + i, 2 * r + hf), device_id_type=MESH
                )

    away = (home != r) | (half != side)
    pl.semaphore_wait(barrier, (nr - 1) + (nc - 1) + (per - 1) + jnp.where(away, 1, 0))

    mine = half * pair + lax.rem(r, pair)
    for o in range(per):
        p = lax.rem(place + o, per)
        send(
            st.at[:, p], s0p.at[half, lax.rem(r, pair)], at["start"] + mine,
            (home, 2 * p + side), away if o == 0 else None,
        )

    @pl.when(jnp.logical_not(away))
    def _():
        s0p[half, lax.rem(r, pair)] = st[:, place]

    for hf in range(2):
        for i in range(pair):
            arrived(
                s0p.at[hf, i], at["start"] + hf * pair + i, (first + i, 2 * r + hf),
                (2 * r + hf != c) | (first + i != r),
            )

    order = [zpeer(o) for o in range(1, nr)] + [r]
    back_order = [r] + [zpeer(o) for o in range(1, nr)]

    def spread(full, name, i, k):
        b, q = first + i, per * k + place
        for o in range(1, nc):
            send(full.at[b, q], full.at[b, q], at[name] + b * nc + q, (r, cpeer(o)))

    def collect(full, name, b, k):
        for o in range(per):
            p = lax.rem(place + o, per)
            q = per * k + p
            arrived(
                full.at[b, q], at[name] + b * nc + q, (r, 2 * p + lax.div(b, pair)),
                lax.div(b, pair) != half if o == 0 else None,
            )

    def mm(a, b, dims):
        return lax.dot_general(a, b, (dims, ((), ())), preferred_element_type=F32)

    def block(full, b, k):
        return full[b, per * k:per * (k + 1)].reshape(rows, df)

    def reduce_rows(full, name, weight, dims, phase, k):
        for o in range(1, nr):
            b = zpeer(o)
            collect(full, name, b, k)
            psend[phase, b, k] = mm(block(full, b, k), weight[...], dims).astype(BF16)
            send(
                psend.at[phase, b, k], zr.at[phase, r, k],
                at[f"zrs{phase}"] + 2 * r + k, (b, c),
            )
        collect(full, name, r, k)
        return mm(block(full, r, k), weight[...], dims)

    def reduced(total, phase, k):
        for o in range(nr - 1, 0, -1):
            b = zpeer(o)
            arrived(zr.at[phase, b, k], at[f"zrs{phase}"] + 2 * b + k, (b, c))
            total = total + zr[phase, b, k].astype(F32)
        return total

    def share_rows(full, phase, k):
        for o in range(1, nr):
            send(full.at[r, k], full.at[r, k], at[f"zag{phase}"] + 2 * r + k, (zpeer(o), c))

    def shared(full, phase, b, k):
        arrived(full.at[b, k], at[f"zag{phase}"] + 2 * b + k, (b, c))

    def group_terms(full, zphase, weight, dims, phase, k):
        for b in [r] + [zpeer(o) for o in range(nr - 1, 0, -1)]:
            if b is not r:
                shared(full, zphase, b, k)
            term = mm(full[b, k], weight[...], dims).astype(BF16)
            ysend[phase, b, per * k:per * (k + 1)] = term.reshape(per, piece, df)
            slot = at[f"crs{phase}"] + (lax.rem(b, pair) * 2 + k) * nc + c
            for o in range(per - 1, -1, -1):
                p = lax.rem(place + o, per)
                send(
                    ysend.at[phase, b, per * k + p], cr.at[phase, lax.rem(b, pair), k, c], slot,
                    (r, 2 * p + lax.div(b, pair)),
                    lax.div(b, pair) != half if o == 0 else None,
                )

    def group_total(phase, i, k):
        total = ysend[phase, first + i, per * k + place].astype(F32)
        for o in range(1, nc):
            j = cpeer(o)
            arrived(cr.at[phase, i, k, j], at[f"crs{phase}"] + (i * 2 + k) * nc + j, (r, j))
            total = total + cr[phase, i, k, j].astype(F32)
        return total

    lane = lax.broadcasted_iota(jnp.int32, (piece, 128), 1)

    def dots(u, k):
        for i in range(pair):
            s = own[u, i, k].astype(F32)
            t = tgp[i, u, k].astype(F32)
            ss = jnp.sum(s * s, axis=-1, keepdims=True)
            sc = jnp.sum(s * t, axis=-1, keepdims=True)
            tt = jnp.sum(t * t, axis=-1, keepdims=True)
            both = jnp.where(lane == 0, ss, jnp.where(lane == 1, sc, tt))
            dsend[u, k, i] = both
            dz[u, k, r, i] = both
        for o in range(1, nr):
            send(dsend.at[u, k], dz.at[u, k, r], at[f"dot{u}"] + 2 * r + k, (zpeer(o), c))

    def dots_in(u, k):
        for o in range(1, nr):
            b = zpeer(o)
            arrived(dz.at[u, k, b], at[f"dot{u}"] + 2 * b + k, (b, c))

    def cosine(u, i, k):
        total = dz[u, k, 0, i]
        for z in range(1, nr):
            total = total + dz[u, k, z, i]
        return cosine_from(
            own[u, i, k].astype(F32), tgp[i, u, k].astype(F32),
            total[:, 0:1], total[:, 1:2], total[:, 2:3],
        )

    ids = lax.broadcasted_iota(jnp.int32, (rows, emb.shape[0]), 1)
    plain, flipped, over_rows = ((1,), (0,)), ((1,), (1,)), ((0,), (0,))

    def into_hidden(u, k):
        total = reduce_rows(sfull.at[u], f"cag{u}", wi, plain, u, k)
        onehot = (act[rows * k:rows * (k + 1), u:u + 1] == ids).astype(F32).astype(BF16)
        pre[u, k] = total + mm(onehot, emb[...], plain)

    def hidden(u, k):
        total = reduced(pre[u, k], u, k)
        pre[u, k] = total
        hfull[u, r, k] = (total * jax.nn.sigmoid(total)).astype(BF16)
        share_rows(hfull.at[u], u, k)

    def next_state(u, k):
        for i in range(pair):
            old = sfull[u, first + i, per * k + place].astype(F32)
            new = (old + group_total(u, i, k)).astype(BF16)
            own[u, i, k] = new
            if u == 0:
                sfull[1, first + i, per * k + place] = new
                spread(sfull.at[1], "cag1", i, k)

    def last_grad(k):
        dots_in(1, k)
        for i in range(pair):
            gfull[1, first + i, per * k + place] = cosine(1, i, k).astype(BF16)
            spread(gfull.at[1], "cag2", i, k)

    def into_back(u, k):
        back[k] = reduce_rows(gfull.at[u], f"cag{3 - u}", wo, flipped, 3 - u, k)

    def hidden_grad(u, k):
        total = reduced(back[k], 3 - u, k)
        efull[u, r, k] = (total * silu_grad(pre[u, k])).astype(BF16)
        share_rows(efull.at[u], 3 - u, k)

    def first_grad(k):
        dots_in(0, k)
        for i in range(pair):
            b, q = first + i, per * k + place
            summed = gfull[1, b, q].astype(F32) + group_total(2, i, k) + cosine(0, i, k)
            gfull[0, b, q] = summed.astype(BF16)
            spread(gfull.at[0], "cag3", i, k)

    back = [None, None]
    for k in range(2):
        for i in range(pair):
            sfull[0, first + i, per * k + place] = jnp.concatenate(
                [s0p[0, i, k], s0p[1, i, k]], axis=-1
            )
            spread(sfull.at[0], "cag0", i, k)
    into_hidden(0, 0)
    into_hidden(0, 1)

    for o in range(1, nr):
        b = zpeer(o)
        send(
            tg.at[:, :, place, :, pl.ds(pl.multiple_of(b * df, df), df)],
            tgp.at[lax.rem(r, pair)], at["targets"] + lax.rem(r, pair), (b, c), side == half,
        )

    @pl.when(side == half)
    def _():
        tgp[lax.rem(r, pair)] = tg[:, :, place, :, pl.ds(pl.multiple_of(r * df, df), df)]

    hidden(0, 0)
    hidden(0, 1)
    group_terms(hfull.at[0], 0, wo, plain, 0, 0)
    next_state(0, 0)
    group_terms(hfull.at[0], 0, wo, plain, 0, 1)
    into_hidden(1, 0)
    next_state(0, 1)
    into_hidden(1, 1)
    for i in range(pair):
        arrived(tgp.at[i], at["targets"] + i, (first + i, c), first + i != r)
    hidden(1, 0)
    hidden(1, 1)
    dots(0, 0)
    dots(0, 1)
    group_terms(hfull.at[1], 1, wo, plain, 1, 0)
    next_state(1, 0)
    dots(1, 0)
    group_terms(hfull.at[1], 1, wo, plain, 1, 1)
    last_grad(0)
    next_state(1, 1)
    dots(1, 1)
    into_back(1, 0)
    last_grad(1)
    into_back(1, 1)
    hidden_grad(1, 0)
    hidden_grad(1, 1)
    group_terms(efull.at[1], 2, wi, flipped, 2, 0)
    first_grad(0)
    group_terms(efull.at[1], 2, wi, flipped, 2, 1)
    into_back(0, 0)
    first_grad(1)
    into_back(0, 1)

    def tall(x):
        return x.reshape(nr * nc * piece, x.shape[-1])

    hidden_grad(0, 0)
    hidden_grad(0, 1)
    gwo[...] = mm(tall(hfull[1]), tall(gfull[1]), over_rows)
    gwi[...] = mm(tall(sfull[1]), tall(efull[1]), over_rows)
    gwo[...] += mm(tall(hfull[0]), tall(gfull[0]), over_rows)
    for k in range(2):
        for b in order[:-1]:
            shared(efull.at[0], 3, b, k)
    gwi[...] += mm(tall(sfull[0]), tall(efull[0]), over_rows)

    for src, dst, sem, slot, dev, when in started:
        if when is None:
            copy(src, dst, sem, slot, dev).wait_send()
        else:
            pl.when(when)(lambda: copy(src, dst, sem, slot, dev).wait_send())


def stationary(nr, nc, state_start, actions, targets, w_in, w_out, action_embed):
    rb, sw = state_start.shape
    piece = rb // nc
    per, pair, rows = nc // 2, nr // 2, rb // 2
    df, fc = w_in.shape
    vm = pl.BlockSpec(memory_space=pltpu.VMEM)
    _, receives = sem_plan(nr, nc)
    return pl.pallas_call(
        functools.partial(kernel, nr, nc),
        out_shape=(
            jax.ShapeDtypeStruct((df, fc), F32),
            jax.ShapeDtypeStruct((fc, df), F32),
        ),
        in_specs=[vm] * 6,
        out_specs=(vm, vm),
        scratch_shapes=[
            pltpu.VMEM((2, pair, 2, piece, sw), BF16),
            pltpu.VMEM((pair, 2, 2, piece, df), BF16),
            pltpu.VMEM((2, nr, nc, piece, df), BF16),
            pltpu.VMEM((2, nr, 2, rows, fc), BF16),
            pltpu.VMEM((2, nr, 2, rows, fc), BF16),
            pltpu.VMEM((2, nr, nc, piece, df), BF16),
            pltpu.VMEM((4, nr, 2, rows, fc), BF16),
            pltpu.VMEM((4, nr, 2, rows, fc), BF16),
            pltpu.VMEM((3, nr, nc, piece, df), BF16),
            pltpu.VMEM((3, pair, 2, nc, piece, df), BF16),
            pltpu.VMEM((2, pair, 2, piece, df), BF16),
            pltpu.VMEM((2, 2, rows, fc), F32),
            pltpu.VMEM((2, 2, pair, piece, 128), F32),
            pltpu.VMEM((2, 2, nr, pair, piece, 128), F32),
            pltpu.SemaphoreType.DMA((sends_in_all(nr, nc),)),
            pltpu.SemaphoreType.DMA((receives,)),
        ],
        compiler_params=pltpu.CompilerParams(
            collective_id=0, has_side_effects=True, vmem_limit_bytes=56 * 1024 * 1024
        ),
    )(
        state_start.reshape(2, per, piece, sw),
        actions,
        targets.reshape(targets.shape[0], 2, per, piece, targets.shape[2]),
        w_in,
        w_out,
        action_embed,
    )


def solution(mesh):
    nr, nc = mesh.shape["row"], mesh.shape["col"]

    def on_device(state_start, actions, targets, w_in, w_out, action_embed):
        rb, sw = state_start.shape
        fits = (
            targets.shape[0] == 2
            and nc == 2 * nr
            and nr % 2 == 0
            and rb % (16 * nc) == 0
            and sw % 128 == 0
            and w_in.shape[0] % 128 == 0
            and w_in.shape[1] % 128 == 0
        )
        args = (state_start, actions, targets, w_in, w_out, action_embed)
        if fits:
            return stationary(nr, nc, *args)
        return gathered(*args)

    in_specs = (
        P("row", "col"),
        P("row", None),
        P(None, "row", None),
        P("row", "col"),
        P("col", "row"),
        P(None, "col"),
    )
    out_specs = (P("row", "col"), P("col", "row"))
    return jax.shard_map(
        on_device, mesh=mesh, in_specs=in_specs, out_specs=out_specs, check_vma=False
    )
```
